32 devices in a mesh: group: 2 (over x), context: 16 (over z, y, core).
Axes of the slice: x: 2, y: 2, z: 4, core: 2. Of those that a mesh axis runs over, the one named last changes fastest.
Arguments:
- features: bfloat16 [4096, 3, 8192], P(('group', 'context')), parts along dimension 0, may hold values from -6 to 6
- base_rows: bfloat16 [4, 3, 8192], replicated, may hold values from -6 to 6
- positions: int32 [128], P('group'), parts along dimension 0, may hold values from 0 to 2047, as said below
- alt_bases: int32 [128], P('group'), parts along dimension 0, may hold values from 0 to 3
- decay_rate: float32 [16, 8192], replicated, may hold values from 9.765625e-06 to 0.03
- residue: float32 [16, 8192], replicated, may hold values from -5 to 5
- skip_gain: float32 [8192], replicated, may hold values from 0.5 to 1.5
Outputs:
- ref_out: bfloat16 [4096, 8192], P(('group', 'context')), parts along dimension 0
- effect: bfloat16 [4096, 8192], P(('group', 'context')), parts along dimension 0
- channel_score: float32 [16384], P(('group', 'context')), parts along dimension 0
The draws below stay inside these ranges and needn't reach their ends.
There are 2 independent parts, one for each index of `group`. The reference program is written for one: setup_inputs(seed, part) draws one part's arguments, and reference() takes and returns one part's arrays. A program takes and returns all parts, laid end to end along the dimension named above; an argument that names none is the same for every part. Nothing has to cross between parts.
Inputs may be any that keep to these rules, and one draw needn't show every extreme that they name: `positions`: ascending; exactly one lies in each aligned stretch of 32 positions; the first is 0 and the last is 2047. `alt_bases`: an index into the first dimension of base_rows.
All inputs are finite; a program needn't handle non-finite values.
Results may differ from the reference program's by a relative error of at most 0.0005.
Values may be sent and summed in bfloat16 or wider, within the bound.
A program may use at most 384 MiB of HBM per device.

```python
import math
import jax
import jax.numpy as jnp
from jax import lax

D = 8192
ORDER = 16
VARS = 64
LEN = 2048


def draw_positions(key, part):
    stride = LEN // VARS
    shifts = jax.random.randint(key, (VARS,), 0, stride)
    ranks = jnp.arange(VARS, dtype=jnp.int32)
    shifts = jnp.where(ranks == 0, 0, jnp.where(ranks == VARS - 1, stride - 1, shifts))
    return (ranks * stride + shifts).astype(jnp.int32)


def plant(values, own_key, least, largest):
    dims = values.shape
    place = [jax.random.randint(jax.random.fold_in(own_key, axis), (), 0, dims[axis]) for axis in range(len(dims))]
    values = values.at[tuple(place)].set(least)
    longest = dims.index(max(dims))
    place[longest] = (place[longest] + 1) % dims[longest]
    return values.at[tuple(place)].set(largest)


def levels(stream_key, dims, cuts, smallest, high):
    def one(axis_at, blocks):
        heights = jax.random.uniform(jax.random.fold_in(jax.random.fold_in(stream_key, 6), axis_at), (blocks,), jnp.float32, smallest / len(cuts), high / len(cuts))
        return jnp.repeat(jnp.exp(heights), dims[axis_at] // blocks).reshape((-1,) + (1,) * (len(dims) - axis_at - 1))

    level = one(*cuts[0])
    for cut in cuts[1:]:
        level = level * one(*cut)
    return level


def scatter_about(rng, shape, scale, limit, shards=(), kind=jnp.bfloat16):
    values = jax.random.normal(rng, shape, jnp.float32) * scale
    if len(shards) > 0:
        values = levels(rng, shape, shards, -0.22, 0.18) * values
    return jnp.clip(values, min=-limit, max=limit).astype(kind)


def setup_inputs(seed: int = 0, part: int = 0) -> dict:
    keys = jax.random.split(jax.random.key(seed), 8)
    part_keys = jax.random.split(jax.random.fold_in(keys[7], part), 8)
    return {
        "features": scatter_about(part_keys[0], (LEN, 3, D), 1.0, 6.0, ((0, 16),)),
        "base_rows": scatter_about(keys[1], (4, 3, D), 1.0, 6.0),
        "positions": draw_positions(jax.random.fold_in(jax.random.fold_in(keys[7], part), 71), part),
        "alt_bases": plant(jax.random.randint(part_keys[3], (VARS,), 0, 4), jax.random.fold_in(part_keys[3], 1), 0, 3).astype(jnp.int32),
        "decay_rate": jnp.clip(jnp.exp(jax.random.uniform(keys[4], (ORDER, D), jnp.float32, math.log(9.765624781721272e-06), math.log(0.03))), 9.765624781721272e-06, 0.03),
        "residue": scatter_about(keys[5], (ORDER, D), 0.35, 5.0, (), jnp.float32),
        "skip_gain": jnp.clip(jax.random.uniform(keys[6], (D,), jnp.float32, 0.5, 1.5), 0.5, 1.5),
    }


def reference(features, base_rows, positions, alt_bases, decay_rate, residue, skip_gain):
    step_decay = jnp.exp(-decay_rate)
    mode_coef = residue * jnp.sqrt(-jnp.expm1(-2.0 * decay_rate))
    variant = features.at[positions].set(base_rows[alt_bases])

    def advance(carry, row_pair):
        modal_state, accum_score = carry
        ref_row, var_row = row_pair
        windows = jnp.stack([ref_row, var_row]).astype(jnp.float32)
        forcing = windows[:, 1] * windows[:, 2]
        modal_state = step_decay[None] * modal_state + forcing[:, None, :]
        filtered = lax.optimization_barrier(jnp.sum(mode_coef[None] * modal_state, axis=1))
        outputs = windows[:, 0] * (filtered + skip_gain[None] * forcing)
        change = outputs[1] - outputs[0]
        return ((modal_state, accum_score + change), (outputs[0].astype(jnp.bfloat16), change.astype(jnp.bfloat16)))
    initial = (jnp.zeros((2, ORDER, D), jnp.float32), jnp.zeros((D,), jnp.float32))
    (_, channel_score), (ref_out, effect) = lax.scan(advance, initial, (features, variant))
    return (ref_out, effect, channel_score)
```

```python
import functools

import jax
import jax.numpy as jnp
import numpy as np
from jax import lax
from jax.experimental import pallas as pl
from jax.experimental.pallas import tpu as pltpu
from jax.sharding import PartitionSpec as P

F32 = jnp.float32
BF16 = jnp.bfloat16
RATE_MAX = 0.03
KD = 10
KB = 7


def cheb_table(length):
    nodes = 64
    theta = (np.arange(nodes) + 0.5) * np.pi / nodes
    rate = (np.cos(theta) + 1.0) * (RATE_MAX / 2)
    values = np.exp(-rate[None] * np.arange(length)[:, None])
    basis = np.cos(np.arange(16)[:, None] * theta[None])
    table = 2.0 / nodes * values @ basis.T
    table[:, 0] *= 0.5
    return table


def split3_lhs(a):
    a = a.astype(np.float32)
    hi = a.astype(jnp.bfloat16)
    lo = (a - hi.astype(np.float32)).astype(jnp.bfloat16)
    return np.concatenate([hi, lo, hi], axis=1)


def split3_rhs(x):
    hi = x.astype(BF16)
    lo = (x - hi.astype(F32)).astype(BF16)
    return jnp.concatenate([hi, hi, lo], axis=0)


def pad_rows(a, rows):
    return np.concatenate([a, np.zeros((rows - a.shape[0],) + a.shape[1:])], axis=0)


def pad_cols(a, cols):
    return np.concatenate([a, np.zeros((a.shape[0], cols - a.shape[1]))], axis=1)


def cheb_terms(rate, count):
    x = rate * (2.0 / RATE_MAX) - 1.0
    terms = [jnp.ones_like(x), x]
    while len(terms) < count:
        terms.append(2.0 * x * terms[-1] - terms[-2])
    return terms


def modal_coef(rate, residue):
    z = 2.0 * rate
    tail = 1.0 - z * (1.0 / 2) * (1.0 - z * (1.0 / 3) * (1.0 - z * (1.0 / 4) * (1.0 - z * (1.0 / 5) * (1.0 - z * (1.0 / 6)))))
    return residue * jnp.sqrt(z * tail)


def moments_kernel(nv, where_ref, alt_ref, gm_ref, k_ref, v_ref, base_ref, out_ref):
    forcing = k_ref[0].astype(F32) * v_ref[0].astype(F32)
    length = forcing.shape[0]
    stretch = length // nv
    moments = jnp.dot(gm_ref[...], split3_rhs(forcing), preferred_element_type=F32)
    table = base_ref[1].astype(F32) * base_ref[2].astype(F32)
    rows = [moments[:KD]]
    step = lax.broadcasted_iota(jnp.int32, (stretch, 1), 0)
    pick = lax.broadcasted_iota(jnp.int32, (table.shape[0], 1), 0)
    for i in range(nv):
        new = jnp.sum(jnp.where(pick == alt_ref[i], table, 0.0), axis=0, keepdims=True)
        part = forcing[i * stretch : (i + 1) * stretch]
        old = jnp.sum(jnp.where(step == where_ref[i], part, 0.0), axis=0, keepdims=True)
        rows.append(new - old)
    rows.append(jnp.zeros((out_ref.shape[1] - KD - nv, forcing.shape[1]), F32))
    packed = jnp.concatenate(rows, axis=0)
    width = out_ref.shape[2]
    for d in range(out_ref.shape[0]):
        out_ref[d] = packed[:, d * width : (d + 1) * width]


def combine_kernel(nv, length, lag_ref, in_ref, rate_ref, residue_ref, out_ref):
    devices = in_ref.shape[0]
    rate = rate_ref[...]
    terms = cheb_terms(rate, KD)
    lead = modal_coef(rate, residue_ref[...]) * jnp.exp(-rate)
    leads = [lead * term for term in terms]
    moments = [in_ref[:, k, :] for k in range(KD)]
    subs = [in_ref[:, KD + i, :] for i in range(nv)]
    lags = [lag_ref[i] for i in range(nv)]
    row = lax.broadcasted_iota(jnp.int32, (devices, in_ref.shape[2]), 0)
    base = [jnp.zeros((devices, in_ref.shape[2]), F32) for _ in range(KD)]
    change = [jnp.zeros((devices, in_ref.shape[2]), F32) for _ in range(KD)]

    def before(ends, rate_n):
        ends = jnp.where(row >= 1, pltpu.roll(ends, 1, 0), 0.0)
        hop = 1
        while hop < devices:
            fade = jnp.exp(rate_n * (-float(length) * hop))
            ends = ends + fade * jnp.where(row >= hop, pltpu.roll(ends, hop, 0), 0.0)
            hop *= 2
        return ends

    for n in range(rate.shape[0]):
        rate_n = rate[n : n + 1]
        ends = terms[0][n : n + 1] * moments[0]
        for k in range(1, KD):
            ends = ends + terms[k][n : n + 1] * moments[k]
        shifted = jnp.exp(-rate_n * lags[0]) * subs[0]
        for i in range(1, nv):
            shifted = shifted + jnp.exp(-rate_n * lags[i]) * subs[i]
        ends, shifted = before(ends, rate_n), before(shifted, rate_n)
        for k in range(KD):
            base[k] = base[k] + leads[k][n : n + 1] * ends
            change[k] = change[k] + leads[k][n : n + 1] * shifted
    for k in range(KD):
        out_ref[:, k, :] = base[k]
        out_ref[:, KD + k, :] = change[k]
    for k in range(2 * KD, out_ref.shape[1]):
        out_ref[:, k, :] = jnp.zeros((devices, in_ref.shape[2]), F32)


def finish_kernel(
    nv, where_ref, alt_ref, gb_ref, gx_ref, gd_ref, q_ref, k_ref, v_ref, base_ref, rate_ref, residue_ref,
    skip_ref, enter_ref, out_ref, effect_ref, score_ref, pad_ref,
):
    length, width = q_ref.shape[1:]
    half, stretch = length // 2, length // nv
    q = q_ref[0].astype(F32)
    forcing = k_ref[0].astype(F32) * v_ref[0].astype(F32)
    skip = skip_ref[...]
    rate = rate_ref[...]
    terms = cheb_terms(rate, KD)
    coef = modal_coef(rate, residue_ref[...])
    lead = coef * jnp.exp(-rate)
    weights = [jnp.sum(coef * term, axis=0, keepdims=True) for term in terms]
    entering = jnp.concatenate([enter_ref[d] for d in range(enter_ref.shape[0])], axis=1)

    filtered = []
    for b in range(2):
        products = jnp.dot(
            gb_ref[...], split3_rhs(forcing[b * half : (b + 1) * half]), preferred_element_type=F32
        )
        total = weights[0] * products[:half]
        for k in range(1, KB):
            total = total + weights[k] * products[k * half : (k + 1) * half]
        filtered.append(total)
        if b == 0:
            first = products[KB * half : KB * half + KB]
    state = terms[0] * first[0:1]
    for k in range(1, KB):
        state = state + terms[k] * first[k : k + 1]
    state = lead * state
    cross = [jnp.sum(terms[k] * state, axis=0, keepdims=True) for k in range(KB)]
    zeros = jnp.zeros((16, width), F32)
    z = jnp.concatenate([entering[:KD], zeros[: 16 - KD]] + cross + [zeros[: 16 - KB]], axis=0)
    filtered = jnp.concatenate(filtered, axis=0) + jnp.dot(
        gx_ref[...], split3_rhs(z), preferred_element_type=F32
    )
    inner = filtered + skip * forcing
    out_ref[...] = (q * inner).astype(out_ref.dtype)

    z = jnp.concatenate([entering[KD : 2 * KD], zeros[: 16 - KD]], axis=0)
    delta = jnp.dot(gd_ref[...], split3_rhs(z), preferred_element_type=F32)
    z = jnp.concatenate(weights + [zeros[: 16 - KD]], axis=0)
    impulse = jnp.dot(gd_ref[...], split3_rhs(z), preferred_element_type=F32)
    for c in range(width // 128):
        pad_ref[c, :length, :] = jnp.zeros((length, 128), F32)
        pad_ref[c, length:, :] = impulse[:, c * 128 : (c + 1) * 128]
    table = base_ref[...].astype(F32)
    step = lax.broadcasted_iota(jnp.int32, (stretch, 1), 0)
    pick = lax.broadcasted_iota(jnp.int32, (table.shape[1], 1), 0)
    deltas = [delta[i * stretch : (i + 1) * stretch] for i in range(nv)]
    total = jnp.zeros((1, width), F32)
    for i in range(nv):
        rows = slice(i * stretch, (i + 1) * stretch)
        hit = step == where_ref[i]
        chosen = pick == alt_ref[i]
        new_q, new_k, new_v = (jnp.sum(jnp.where(chosen, table[j], 0.0), axis=0, keepdims=True) for j in range(3))
        force_step = jnp.where(hit, new_k * new_v - forcing[rows], 0.0)
        gate_step = jnp.where(hit, new_q - q[rows], 0.0)
        impact = jnp.sum(force_step, axis=0, keepdims=True)
        place = where_ref[i]
        for j in range(i, nv):
            response = jnp.concatenate(
                [
                    pad_ref[c, pl.ds(length + (j - i) * stretch - place, stretch), :]
                    for c in range(width // 128)
                ],
                axis=1,
            )
            deltas[j] = deltas[j] + response * impact
        change = (q[rows] + gate_step) * (deltas[i] + skip * force_step) + gate_step * inner[rows]
        effect_ref[rows, :] = change.astype(effect_ref.dtype)
        total = total + jnp.sum(change, axis=0, keepdims=True)
    score_ref[...] = total


def exchange(blocks):
    return lax.all_to_all(blocks, "context", 0, 0, tiled=True)


def on_device(features, base_rows, positions, alt_bases, decay_rate, residue, skip_gain):
    length, _, width = features.shape
    modes = decay_rate.shape[0]
    devices = lax.axis_size("context")
    me = lax.axis_index("context")
    nv = positions.shape[0] // devices
    share = width // devices
    half, stretch = length // 2, length // nv
    table = cheb_table(length)

    rows = features.transpose(1, 0, 2)
    bases = base_rows.transpose(1, 0, 2)
    local = positions.reshape(devices, nv) - jnp.arange(devices, dtype=jnp.int32)[:, None] * length
    within = local - jnp.arange(nv, dtype=jnp.int32)[None] * stretch
    my_within = lax.dynamic_index_in_dim(within, me, 0, keepdims=False)
    my_alt = lax.dynamic_slice_in_dim(alt_bases, me * nv, nv)
    lags = (length - 1 - local).astype(F32).T
    lags = jnp.broadcast_to(lags[:, :, None], (nv, devices, 128))

    smem = pl.BlockSpec(memory_space=pltpu.SMEM)
    parallel = pltpu.CompilerParams(dimension_semantics=("arbitrary",))

    def row_spec(index, chunk):
        return pl.BlockSpec((1, length, chunk), lambda j, index=index: (index, 0, j))

    def whole(a):
        return pl.BlockSpec(a.shape, lambda j: (0,) * a.ndim)

    gm = jnp.asarray(split3_lhs(pad_rows(table[::-1, :KD].T, 16)))
    chunk = 1024
    sends = pl.pallas_call(
        functools.partial(moments_kernel, nv),
        grid=(width // chunk,),
        in_specs=[
            smem, smem, whole(gm), row_spec(1, chunk), row_spec(2, chunk),
            pl.BlockSpec((3, bases.shape[1], chunk), lambda j: (0, 0, j)),
        ],
        out_specs=pl.BlockSpec((chunk // share, 16, share), lambda j: (j, 0, 0)),
        out_shape=jax.ShapeDtypeStruct((devices, 16, share), F32),
        compiler_params=parallel,
        name="moments",
    )(my_within, my_alt, gm, rows, rows, bases)

    got = exchange(sends)
    my_rate = lax.dynamic_slice_in_dim(decay_rate, me * share, share, axis=1)
    my_residue = lax.dynamic_slice_in_dim(residue, me * share, share, axis=1)
    back = pl.pallas_call(
        functools.partial(combine_kernel, nv, length),
        grid=(share // 128,),
        in_specs=[
            whole(lags),
            pl.BlockSpec((devices, 16, 128), lambda j: (0, 0, j)),
            pl.BlockSpec((modes, 128), lambda j: (0, j)),
            pl.BlockSpec((modes, 128), lambda j: (0, j)),
        ],
        out_specs=pl.BlockSpec((devices, 24, 128), lambda j: (0, 0, j)),
        out_shape=jax.ShapeDtypeStruct((devices, 24, share), F32),
        compiler_params=parallel,
        name="combine",
    )(lags, got, my_rate, my_residue)
    entering = exchange(back)

    lag = np.arange(half)[:, None] - np.arange(half)[None]
    toeplitz = np.where((lag >= 0)[None], table[np.maximum(lag, 0), :KB].transpose(2, 0, 1), 0.0)
    toeplitz = toeplitz.reshape(KB * half, half)
    ends = pad_rows(table[:half, :KB][::-1].T, 8)
    gb = jnp.asarray(split3_lhs(np.concatenate([toeplitz, ends], axis=0)))
    late = np.concatenate([np.zeros((half, 16)), pad_cols(table[:half, :KB], 16)], axis=0)
    gx = jnp.asarray(split3_lhs(np.concatenate([pad_cols(table[:, :KD], 16), late], axis=1)))
    gd = jnp.asarray(split3_lhs(pad_cols(table[:, :KD], 16)))
    chunk = 512
    ref_out, effect, score_part = pl.pallas_call(
        functools.partial(finish_kernel, nv),
        grid=(width // chunk,),
        in_specs=[
            smem, smem, whole(gb), whole(gx), whole(gd),
            row_spec(0, chunk), row_spec(1, chunk), row_spec(2, chunk),
            pl.BlockSpec((3, bases.shape[1], chunk), lambda j: (0, 0, j)),
            pl.BlockSpec((modes, chunk), lambda j: (0, j)),
            pl.BlockSpec((modes, chunk), lambda j: (0, j)),
            pl.BlockSpec((1, chunk), lambda j: (0, j)),
            pl.BlockSpec((chunk // share, 24, share), lambda j: (j, 0, 0)),
        ],
        out_specs=[
            pl.BlockSpec((length, chunk), lambda j: (0, j)),
            pl.BlockSpec((length, chunk), lambda j: (0, j)),
            pl.BlockSpec((1, chunk), lambda j: (0, j)),
        ],
        out_shape=[
            jax.ShapeDtypeStruct((length, width), BF16),
            jax.ShapeDtypeStruct((length, width), BF16),
            jax.ShapeDtypeStruct((1, width), F32),
        ],
        scratch_shapes=[pltpu.VMEM((chunk // 128, 2 * length, 128), F32)],
        compiler_params=parallel,
        name="finish",
    )(
        my_within, my_alt, gb, gx, gd, rows, rows, rows, bases, decay_rate, residue,
        skip_gain.reshape(1, width), entering,
    )
    channel_score = lax.psum_scatter(score_part[0], "context", scatter_dimension=0, tiled=True)
    return ref_out, effect, channel_score


def solution(mesh):
    return jax.shard_map(
        on_device,
        mesh=mesh,
        in_specs=(P(("group", "context"), None, None), P(), P("group"), P("group"), P(), P(), P()),
        out_specs=(
            P(("group", "context"), None),
            P(("group", "context"), None),
            P(("group", "context")),
        ),
        check_vma=False,
    )
```

```python
import functools

import jax
import jax.numpy as jnp
import numpy as np
from jax import lax
from jax.experimental import pallas as pl
from jax.experimental.pallas import tpu as pltpu
from jax.sharding import PartitionSpec as P

F32 = jnp.float32
BF16 = jnp.bfloat16
MESH = pl.DeviceIdType.MESH
RATE_MAX = 0.03
KD = 10
KB = 7


def cheb_table(length):
    nodes = 64
    theta = (np.arange(nodes) + 0.5) * np.pi / nodes
    rate = (np.cos(theta) + 1.0) * (RATE_MAX / 2)
    values = np.exp(-rate[None] * np.arange(length)[:, None])
    basis = np.cos(np.arange(16)[:, None] * theta[None])
    table = 2.0 / nodes * values @ basis.T
    table[:, 0] *= 0.5
    return table


def split3_lhs(a):
    a = a.astype(np.float32)
    hi = a.astype(jnp.bfloat16)
    lo = (a - hi.astype(np.float32)).astype(jnp.bfloat16)
    return np.concatenate([hi, lo, hi], axis=1)


def split3_rhs(x):
    hi = x.astype(BF16)
    lo = (x - hi.astype(F32)).astype(BF16)
    return jnp.concatenate([hi, hi, lo], axis=0)


def pad_rows(a, rows):
    return np.concatenate([a, np.zeros((rows - a.shape[0],) + a.shape[1:])], axis=0)


def pad_cols(a, cols):
    return np.concatenate([a, np.zeros((a.shape[0], cols - a.shape[1]))], axis=1)


def cheb_terms(rate, count):
    x = rate * (2.0 / RATE_MAX) - 1.0
    terms = [jnp.ones_like(x), x]
    while len(terms) < count:
        terms.append(2.0 * x * terms[-1] - terms[-2])
    return terms


def modal_coef(rate, residue):
    z = 2.0 * rate
    tail = 1.0 - z * (1.0 / 2) * (1.0 - z * (1.0 / 3) * (1.0 - z * (1.0 / 4) * (1.0 - z * (1.0 / 5) * (1.0 - z * (1.0 / 6)))))
    return residue * jnp.sqrt(z * tail)


def moments_kernel(nv, where_ref, alt_ref, gm_ref, k_ref, v_ref, base_ref, out_ref):
    forcing = k_ref[0].astype(F32) * v_ref[0].astype(F32)
    length = forcing.shape[0]
    stretch = length // nv
    moments = jnp.dot(gm_ref[...], split3_rhs(forcing), preferred_element_type=F32)
    table = base_ref[1].astype(F32) * base_ref[2].astype(F32)
    rows = [moments[:KD]]
    step = lax.broadcasted_iota(jnp.int32, (stretch, 1), 0)
    pick = lax.broadcasted_iota(jnp.int32, (table.shape[0], 1), 0)
    for i in range(nv):
        new = jnp.sum(jnp.where(pick == alt_ref[i], table, 0.0), axis=0, keepdims=True)
        part = forcing[i * stretch : (i + 1) * stretch]
        old = jnp.sum(jnp.where(step == where_ref[i], part, 0.0), axis=0, keepdims=True)
        rows.append(new - old)
    packed = jnp.concatenate(rows, axis=0)
    height = packed.shape[0]
    tiles = out_ref.shape[1] // height
    for d in range(out_ref.shape[0]):
        for c in range(tiles):
            lanes = (d * tiles + c) * 128
            out_ref[d, c * height : (c + 1) * height, :] = packed[:, lanes : lanes + 128]


def combine(nv, length, lag_ref, in_ref, rate_ref, residue_ref, out_ref):
    devices = in_ref.shape[0]
    height = KD + nv
    row = lax.broadcasted_iota(jnp.int32, (devices, 128), 0)

    def before(ends, rate_n):
        ends = jnp.where(row >= 1, pltpu.roll(ends, 1, 0), 0.0)
        hop = 1
        while hop < devices:
            fade = jnp.exp(rate_n * (-float(length) * hop))
            ends = ends + fade * jnp.where(row >= hop, pltpu.roll(ends, hop, 0), 0.0)
            hop *= 2
        return ends

    for c in range(rate_ref.shape[1] // 128):
        rate = rate_ref[:, c * 128 : (c + 1) * 128]
        terms = cheb_terms(rate, KD)
        lead = modal_coef(rate, residue_ref[:, c * 128 : (c + 1) * 128]) * jnp.exp(-rate)
        leads = [lead * term for term in terms]
        moments = [in_ref[:, c * height + k, :] for k in range(KD)]
        subs = [in_ref[:, c * height + KD + i, :] for i in range(nv)]
        lags = [lag_ref[i] for i in range(nv)]
        base = [jnp.zeros((devices, 128), F32) for _ in range(KD)]
        change = [jnp.zeros((devices, 128), F32) for _ in range(KD)]
        for n in range(rate.shape[0]):
            rate_n = rate[n : n + 1]
            ends = terms[0][n : n + 1] * moments[0]
            for k in range(1, KD):
                ends = ends + terms[k][n : n + 1] * moments[k]
            shifted = jnp.exp(-rate_n * lags[0]) * subs[0]
            for i in range(1, nv):
                shifted = shifted + jnp.exp(-rate_n * lags[i]) * subs[i]
            ends, shifted = before(ends, rate_n), before(shifted, rate_n)
            for k in range(KD):
                base[k] = base[k] + leads[k][n : n + 1] * ends
                change[k] = change[k] + leads[k][n : n + 1] * shifted
        for k in range(KD):
            out_ref[:, c * 2 * KD + k, :] = base[k]
            out_ref[:, c * 2 * KD + KD + k, :] = change[k]


def greet(devices):
    me = lax.axis_index("context")
    barrier = pltpu.get_barrier_semaphore()
    for hop in range(1, devices):
        pl.semaphore_signal(
            barrier, inc=1, device_id={"context": lax.rem(me + hop, devices)}, device_id_type=MESH
        )
    pl.semaphore_wait(barrier, devices - 1)


def hand_out(src_ref, dst_ref, own_sem, send_sems, recv_sems):
    devices = src_ref.shape[0]
    me = lax.axis_index("context")
    copies = []
    for hop in range(1, devices):
        peer = lax.rem(me + hop, devices)
        copies.append(
            pltpu.make_async_remote_copy(
                src_ref=src_ref.at[peer],
                dst_ref=dst_ref.at[me],
                send_sem=send_sems.at[hop],
                recv_sem=recv_sems.at[hop],
                device_id={"context": peer},
                device_id_type=MESH,
            )
        )
        copies[-1].start()
    own = pltpu.make_async_copy(src_ref.at[me], dst_ref.at[me], own_sem)
    own.start()
    return copies + [own]


def route_kernel(
    nv, length, lag_ref, mine_ref, rate_ref, residue_ref, out_ref,
    got_ref, back_ref, own_sems, send_sems, recv_sems,
):
    greet(mine_ref.shape[0])
    for copy in hand_out(mine_ref, got_ref, own_sems.at[0], send_sems.at[0], recv_sems.at[0]):
        copy.wait()
    combine(nv, length, lag_ref, got_ref, rate_ref, residue_ref, back_ref)
    for copy in hand_out(back_ref, out_ref, own_sems.at[1], send_sems.at[1], recv_sems.at[1]):
        copy.wait()


def score_kernel(parts_ref, out_ref, got_ref, own_sem, send_sems, recv_sems):
    greet(parts_ref.shape[0])
    for copy in hand_out(parts_ref, got_ref, own_sem, send_sems, recv_sems):
        copy.wait()
    out_ref[...] = jnp.sum(got_ref[...], axis=0)


def finish_kernel(
    nv, where_ref, alt_ref, gb_ref, gx_ref, gd_ref, q_ref, k_ref, v_ref, base_ref, rate_ref, residue_ref,
    skip_ref, enter_ref, out_ref, effect_ref, score_ref, pad_ref,
):
    length, width = q_ref.shape[1:]
    half, stretch = length // 2, length // nv
    q = q_ref[0].astype(F32)
    forcing = k_ref[0].astype(F32) * v_ref[0].astype(F32)
    skip = skip_ref[...]
    rate = rate_ref[...]
    terms = cheb_terms(rate, KD)
    coef = modal_coef(rate, residue_ref[...])
    lead = coef * jnp.exp(-rate)
    weights = [jnp.sum(coef * term, axis=0, keepdims=True) for term in terms]
    entering = jnp.concatenate(
        [
            enter_ref[d, c : c + 2 * KD, :]
            for d in range(enter_ref.shape[0])
            for c in range(0, enter_ref.shape[1], 2 * KD)
        ],
        axis=1,
    )

    filtered = []
    for b in range(2):
        products = jnp.dot(
            gb_ref[...], split3_rhs(forcing[b * half : (b + 1) * half]), preferred_element_type=F32
        )
        total = weights[0] * products[:half]
        for k in range(1, KB):
            total = total + weights[k] * products[k * half : (k + 1) * half]
        filtered.append(total)
        if b == 0:
            first = products[KB * half : KB * half + KB]
    state = terms[0] * first[0:1]
    for k in range(1, KB):
        state = state + terms[k] * first[k : k + 1]
    state = lead * state
    cross = [jnp.sum(terms[k] * state, axis=0, keepdims=True) for k in range(KB)]
    zeros = jnp.zeros((16, width), F32)
    z = jnp.concatenate([entering[:KD], zeros[: 16 - KD]] + cross + [zeros[: 16 - KB]], axis=0)
    filtered = jnp.concatenate(filtered, axis=0) + jnp.dot(
        gx_ref[...], split3_rhs(z), preferred_element_type=F32
    )
    inner = filtered + skip * forcing
    out_ref[...] = (q * inner).astype(out_ref.dtype)

    z = jnp.concatenate([entering[KD : 2 * KD], zeros[: 16 - KD]], axis=0)
    delta = jnp.dot(gd_ref[...], split3_rhs(z), preferred_element_type=F32)
    z = jnp.concatenate(weights + [zeros[: 16 - KD]], axis=0)
    impulse = jnp.dot(gd_ref[...], split3_rhs(z), preferred_element_type=F32)
    for c in range(width // 128):
        pad_ref[c, :length, :] = jnp.zeros((length, 128), F32)
        pad_ref[c, length:, :] = impulse[:, c * 128 : (c + 1) * 128]
    table = base_ref[...].astype(F32)
    step = lax.broadcasted_iota(jnp.int32, (stretch, 1), 0)
    pick = lax.broadcasted_iota(jnp.int32, (table.shape[1], 1), 0)
    deltas = [delta[i * stretch : (i + 1) * stretch] for i in range(nv)]
    total = jnp.zeros((1, width), F32)
    for i in range(nv):
        rows = slice(i * stretch, (i + 1) * stretch)
        hit = step == where_ref[i]
        chosen = pick == alt_ref[i]
        new_q, new_k, new_v = (jnp.sum(jnp.where(chosen, table[j], 0.0), axis=0, keepdims=True) for j in range(3))
        force_step = jnp.where(hit, new_k * new_v - forcing[rows], 0.0)
        gate_step = jnp.where(hit, new_q - q[rows], 0.0)
        impact = jnp.sum(force_step, axis=0, keepdims=True)
        place = where_ref[i]
        for j in range(i, nv):
            response = jnp.concatenate(
                [
                    pad_ref[c, pl.ds(length + (j - i) * stretch - place, stretch), :]
                    for c in range(width // 128)
                ],
                axis=1,
            )
            deltas[j] = deltas[j] + response * impact
        change = (q[rows] + gate_step) * (deltas[i] + skip * force_step) + gate_step * inner[rows]
        effect_ref[rows, :] = change.astype(effect_ref.dtype)
        total = total + jnp.sum(change, axis=0, keepdims=True)
    score_ref[...] = total


def on_device(features, base_rows, positions, alt_bases, decay_rate, residue, skip_gain):
    length, _, width = features.shape
    modes = decay_rate.shape[0]
    devices = lax.axis_size("context")
    me = lax.axis_index("context")
    nv = positions.shape[0] // devices
    share = width // devices
    tiles = share // 128
    half, stretch = length // 2, length // nv
    table = cheb_table(length)

    rows = features.transpose(1, 0, 2)
    bases = base_rows.transpose(1, 0, 2)
    local = positions.reshape(devices, nv) - jnp.arange(devices, dtype=jnp.int32)[:, None] * length
    within = local - jnp.arange(nv, dtype=jnp.int32)[None] * stretch
    my_within = lax.dynamic_index_in_dim(within, me, 0, keepdims=False)
    my_alt = lax.dynamic_slice_in_dim(alt_bases, me * nv, nv)
    lags = (length - 1 - local).astype(F32).T
    lags = jnp.broadcast_to(lags[:, :, None], (nv, devices, 128))

    smem = pl.BlockSpec(memory_space=pltpu.SMEM)
    parallel = pltpu.CompilerParams(dimension_semantics=("arbitrary",))

    def row_spec(index, chunk):
        return pl.BlockSpec((1, length, chunk), lambda j, index=index: (index, 0, j))

    def whole(a):
        return pl.BlockSpec(a.shape, lambda j: (0,) * a.ndim)

    gm = jnp.asarray(split3_lhs(pad_rows(table[::-1, :KD].T, 16)))
    chunk = 1024
    sends = pl.pallas_call(
        functools.partial(moments_kernel, nv),
        grid=(width // chunk,),
        in_specs=[
            smem, smem, whole(gm), row_spec(1, chunk), row_spec(2, chunk),
            pl.BlockSpec((3, bases.shape[1], chunk), lambda j: (0, 0, j)),
        ],
        out_specs=pl.BlockSpec((chunk // share, tiles * (KD + nv), 128), lambda j: (j, 0, 0)),
        out_shape=jax.ShapeDtypeStruct((devices, tiles * (KD + nv), 128), F32),
        compiler_params=parallel,
        name="moments",
    )(my_within, my_alt, gm, rows, rows, bases)

    my_rate = lax.dynamic_slice_in_dim(decay_rate, me * share, share, axis=1)
    my_residue = lax.dynamic_slice_in_dim(residue, me * share, share, axis=1)
    vmem = pl.BlockSpec(memory_space=pltpu.VMEM)
    entering = pl.pallas_call(
        functools.partial(route_kernel, nv, length),
        in_specs=[vmem] * 4,
        out_specs=vmem,
        out_shape=jax.ShapeDtypeStruct((devices, tiles * 2 * KD, 128), F32),
        scratch_shapes=[
            pltpu.VMEM((devices, tiles * (KD + nv), 128), F32),
            pltpu.VMEM((devices, tiles * 2 * KD, 128), F32),
            pltpu.SemaphoreType.DMA((2,)),
            pltpu.SemaphoreType.DMA((2, devices)),
            pltpu.SemaphoreType.DMA((2, devices)),
        ],
        compiler_params=pltpu.CompilerParams(collective_id=0, has_side_effects=True),
        name="route",
    )(lags, sends, my_rate, my_residue)

    lag = np.arange(half)[:, None] - np.arange(half)[None]
    toeplitz = np.where((lag >= 0)[None], table[np.maximum(lag, 0), :KB].transpose(2, 0, 1), 0.0)
    toeplitz = toeplitz.reshape(KB * half, half)
    ends = pad_rows(table[:half, :KB][::-1].T, 8)
    gb = jnp.asarray(split3_lhs(np.concatenate([toeplitz, ends], axis=0)))
    late = np.concatenate([np.zeros((half, 16)), pad_cols(table[:half, :KB], 16)], axis=0)
    gx = jnp.asarray(split3_lhs(np.concatenate([pad_cols(table[:, :KD], 16), late], axis=1)))
    gd = jnp.asarray(split3_lhs(pad_cols(table[:, :KD], 16)))
    chunk = 512
    ref_out, effect, score_part = pl.pallas_call(
        functools.partial(finish_kernel, nv),
        grid=(width // chunk,),
        in_specs=[
            smem, smem, whole(gb), whole(gx), whole(gd),
            row_spec(0, chunk), row_spec(1, chunk), row_spec(2, chunk),
            pl.BlockSpec((3, bases.shape[1], chunk), lambda j: (0, 0, j)),
            pl.BlockSpec((modes, chunk), lambda j: (0, j)),
            pl.BlockSpec((modes, chunk), lambda j: (0, j)),
            pl.BlockSpec((1, chunk), lambda j: (0, j)),
            pl.BlockSpec((chunk // share, tiles * 2 * KD, 128), lambda j: (j, 0, 0)),
        ],
        out_specs=[
            pl.BlockSpec((length, chunk), lambda j: (0, j)),
            pl.BlockSpec((length, chunk), lambda j: (0, j)),
            pl.BlockSpec((1, chunk), lambda j: (0, j)),
        ],
        out_shape=[
            jax.ShapeDtypeStruct((length, width), BF16),
            jax.ShapeDtypeStruct((length, width), BF16),
            jax.ShapeDtypeStruct((1, width), F32),
        ],
        scratch_shapes=[pltpu.VMEM((chunk // 128, 2 * length, 128), F32)],
        compiler_params=parallel,
        name="finish",
    )(
        my_within, my_alt, gb, gx, gd, rows, rows, rows, bases, decay_rate, residue,
        skip_gain.reshape(1, width), entering,
    )
    channel_score = pl.pallas_call(
        score_kernel,
        in_specs=[vmem],
        out_specs=vmem,
        out_shape=jax.ShapeDtypeStruct((tiles, 128), F32),
        scratch_shapes=[
            pltpu.VMEM((devices, tiles, 128), F32),
            pltpu.SemaphoreType.DMA,
            pltpu.SemaphoreType.DMA((devices,)),
            pltpu.SemaphoreType.DMA((devices,)),
        ],
        compiler_params=pltpu.CompilerParams(collective_id=1, has_side_effects=True),
        name="score",
    )(score_part.reshape(devices, tiles, 128))
    return ref_out, effect, channel_score.reshape(share)


def solution(mesh):
    return jax.shard_map(
        on_device,
        mesh=mesh,
        in_specs=(P(("group", "context"), None, None), P(), P("group"), P("group"), P(), P(), P()),
        out_specs=(
            P(("group", "context"), None),
            P(("group", "context"), None),
            P(("group", "context")),
        ),
        check_vma=False,
    )
```

```python
import functools

import jax
import jax.numpy as jnp
import numpy as np
from jax import lax
from jax.experimental import pallas as pl
from jax.experimental.pallas import tpu as pltpu
from jax.sharding import PartitionSpec as P

F32 = jnp.float32
BF16 = jnp.bfloat16
MESH = pl.DeviceIdType.MESH
RATE_MAX = 0.03
KD = 10
KB = 7


def cheb_table(length):
    nodes = 64
    theta = (np.arange(nodes) + 0.5) * np.pi / nodes
    rate = (np.cos(theta) + 1.0) * (RATE_MAX / 2)
    values = np.exp(-rate[None] * np.arange(length)[:, None])
    basis = np.cos(np.arange(16)[:, None] * theta[None])
    table = 2.0 / nodes * values @ basis.T
    table[:, 0] *= 0.5
    return table


def split3_lhs(a):
    a = a.astype(np.float32)
    hi = a.astype(jnp.bfloat16)
    lo = (a - hi.astype(np.float32)).astype(jnp.bfloat16)
    return np.concatenate([hi, lo, hi], axis=1)


def split3_rhs(x):
    hi = x.astype(BF16)
    lo = (x - hi.astype(F32)).astype(BF16)
    return jnp.concatenate([hi, hi, lo], axis=0)


def pad_rows(a, rows):
    return np.concatenate([a, np.zeros((rows - a.shape[0],) + a.shape[1:])], axis=0)


def pad_cols(a, cols):
    return np.concatenate([a, np.zeros((a.shape[0], cols - a.shape[1]))], axis=1)


def cheb_terms(rate, count):
    x = rate * (2.0 / RATE_MAX) - 1.0
    terms = [jnp.ones_like(x), x]
    while len(terms) < count:
        terms.append(2.0 * x * terms[-1] - terms[-2])
    return terms


def modal_coef(rate, residue):
    z = 2.0 * rate
    tail = 1.0 - z * (1.0 / 2) * (1.0 - z * (1.0 / 3) * (1.0 - z * (1.0 / 4) * (1.0 - z * (1.0 / 5) * (1.0 - z * (1.0 / 6)))))
    return residue * jnp.sqrt(z * tail)


def combine(nv, length, lags, in_ref, my_rate, my_residue, out_ref):
    devices = in_ref.shape[0]
    height = KD + nv
    row = lax.broadcasted_iota(jnp.int32, (devices, 128), 0)

    def before(ends, rate_n):
        ends = jnp.where(row >= 1, pltpu.roll(ends, 1, 0), 0.0)
        hop = 1
        while hop < devices:
            fade = jnp.exp(rate_n * (-float(length) * hop))
            ends = ends + fade * jnp.where(row >= hop, pltpu.roll(ends, hop, 0), 0.0)
            hop *= 2
        return ends

    for c in range(my_rate.shape[1] // 128):
        rate = my_rate[:, c * 128 : (c + 1) * 128]
        terms = cheb_terms(rate, KD)
        lead = modal_coef(rate, my_residue[:, c * 128 : (c + 1) * 128]) * jnp.exp(-rate)
        leads = [lead * term for term in terms]
        moments = [in_ref[:, c * height + k, :] for k in range(KD)]
        subs = [in_ref[:, c * height + KD + i, :] for i in range(nv)]
        base = [jnp.zeros((devices, 128), F32) for _ in range(KD)]
        change = [jnp.zeros((devices, 128), F32) for _ in range(KD)]
        for n in range(rate.shape[0]):
            rate_n = rate[n : n + 1]
            ends = terms[0][n : n + 1] * moments[0]
            for k in range(1, KD):
                ends = ends + terms[k][n : n + 1] * moments[k]
            shifted = jnp.exp(-rate_n * lags[0]) * subs[0]
            for i in range(1, nv):
                shifted = shifted + jnp.exp(-rate_n * lags[i]) * subs[i]
            ends, shifted = before(ends, rate_n), before(shifted, rate_n)
            for k in range(KD):
                base[k] = base[k] + leads[k][n : n + 1] * ends
                change[k] = change[k] + leads[k][n : n + 1] * shifted
        for k in range(KD):
            out_ref[:, c * 2 * KD + k, :] = base[k]
            out_ref[:, c * 2 * KD + KD + k, :] = change[k]


def greet(devices):
    me = lax.axis_index("context")
    barrier = pltpu.get_barrier_semaphore()
    for hop in range(1, devices):
        pl.semaphore_signal(
            barrier, inc=1, device_id={"context": lax.rem(me + hop, devices)}, device_id_type=MESH
        )
    return lambda: pl.semaphore_wait(barrier, devices - 1)


def hand_out(src_ref, dst_ref, own_sem, send_sems, recv_sems):
    devices = src_ref.shape[0]
    me = lax.axis_index("context")
    copies = []
    for hop in range(1, devices):
        peer = lax.rem(me + hop, devices)
        copies.append(
            pltpu.make_async_remote_copy(
                src_ref=src_ref.at[peer],
                dst_ref=dst_ref.at[me],
                send_sem=send_sems.at[hop],
                recv_sem=recv_sems.at[hop],
                device_id={"context": peer},
                device_id_type=MESH,
            )
        )
        copies[-1].start()
    own = pltpu.make_async_copy(src_ref.at[me], dst_ref.at[me], own_sem)
    own.start()
    return copies + [own]


def kernel(
    nv, pos_ref, alt_ref, gm_ref, gb_ref, gx_ref, gd_ref, rows_ref, base_ref, rate_ref, residue_ref, skip_ref,
    out_ref, effect_ref, score_ref,
    mine_ref, got_ref, back_ref, enter_ref, inner_ref, delta_ref, pad_ref, parts_ref, sums_ref,
    own_sems, send_sems, recv_sems,
):
    length, width = out_ref.shape
    devices, me = lax.axis_size("context"), lax.axis_index("context")
    share = width // devices
    tiles = share // 128
    half, stretch = length // 2, length // nv
    chunk = 512
    chunks, owners = width // chunk, chunk // share
    step = lax.broadcasted_iota(jnp.int32, (stretch, 1), 0)
    pick = lax.broadcasted_iota(jnp.int32, (base_ref.shape[1], 1), 0)
    places = [lax.rem(pos_ref[me * nv + i], stretch) for i in range(nv)]
    alts = [alt_ref[me * nv + i] for i in range(nv)]
    slabs = [slice(i * stretch, (i + 1) * stretch) for i in range(nv)]

    def columns(j):
        return pl.ds(pl.multiple_of(j * chunk, chunk), chunk)

    def force(cols):
        return rows_ref[1, :, cols].astype(F32) * rows_ref[2, :, cols].astype(F32)

    def force_steps(forcing, cols):
        table = base_ref[1, :, cols].astype(F32) * base_ref[2, :, cols].astype(F32)
        steps = []
        for i in range(nv):
            new = jnp.sum(jnp.where(pick == alts[i], table, 0.0), axis=0, keepdims=True)
            steps.append(jnp.where(step == places[i], new - forcing[slabs[i]], 0.0))
        return steps

    barrier_wait = greet(devices)

    def moments(j, carry):
        cols = columns(j)
        forcing = force(cols)
        sums = jnp.dot(gm_ref[...], split3_rhs(forcing), preferred_element_type=F32)
        steps = [jnp.sum(part, axis=0, keepdims=True) for part in force_steps(forcing, cols)]
        packed = jnp.concatenate([sums[:KD]] + steps, axis=0)
        for d in range(owners):
            for c in range(tiles):
                lanes = (d * tiles + c) * 128
                mine_ref[j * owners + d, c * (KD + nv) : (c + 1) * (KD + nv), :] = packed[:, lanes : lanes + 128]
        return carry

    lax.fori_loop(0, chunks, moments, 0)
    barrier_wait()
    first_leg = hand_out(mine_ref, got_ref, own_sems.at[0], send_sems.at[0], recv_sems.at[0])

    def local(j, carry):
        cols = columns(j)
        forcing = force(cols)
        skip = skip_ref[:, cols]
        rate = rate_ref[:, cols]
        terms = cheb_terms(rate, KD)
        coef = modal_coef(rate, residue_ref[:, cols])
        lead = coef * jnp.exp(-rate)
        weights = [jnp.sum(coef * term, axis=0, keepdims=True) for term in terms]
        filtered = []
        for b in range(2):
            products = jnp.dot(
                gb_ref[...], split3_rhs(forcing[b * half : (b + 1) * half]), preferred_element_type=F32
            )
            total = weights[0] * products[:half]
            for k in range(1, KB):
                total = total + weights[k] * products[k * half : (k + 1) * half]
            filtered.append(total)
            if b == 0:
                first = products[KB * half : KB * half + KB]
        state = terms[0] * first[0:1]
        for k in range(1, KB):
            state = state + terms[k] * first[k : k + 1]
        state = lead * state
        zeros = jnp.zeros((16, chunk), F32)
        cross = [jnp.sum(terms[k] * state, axis=0, keepdims=True) for k in range(KB)]
        z = jnp.concatenate(cross + [zeros[: 16 - KB]], axis=0)
        filtered[1] = filtered[1] + jnp.dot(gx_ref[...], split3_rhs(z), preferred_element_type=F32)
        inner_ref[:, cols] = jnp.concatenate(filtered, axis=0) + skip * forcing

        z = jnp.concatenate(weights + [zeros[: 16 - KD]], axis=0)
        impulse = jnp.dot(gd_ref[...], split3_rhs(z), preferred_element_type=F32)
        for c in range(chunk // 128):
            pad_ref[c, length:, :] = impulse[:, c * 128 : (c + 1) * 128]
        steps = force_steps(forcing, cols)
        deltas = [skip * part for part in steps]
        for i in range(nv):
            impact = jnp.sum(steps[i], axis=0, keepdims=True)
            for j2 in range(i, nv):
                response = jnp.concatenate(
                    [
                        pad_ref[c, pl.ds(length + (j2 - i) * stretch - places[i], stretch), :]
                        for c in range(chunk // 128)
                    ],
                    axis=1,
                )
                deltas[j2] = deltas[j2] + response * impact
        for i in range(nv):
            delta_ref[slabs[i], cols] = deltas[i]
        return carry

    for c in range(chunk // 128):
        pad_ref[c, :length, :] = jnp.zeros((length, 128), F32)
    early = chunks // 2
    lax.fori_loop(0, early, local, 0)

    for copy in first_leg:
        copy.wait()
    mine = pl.ds(pl.multiple_of(me * share, share), share)
    row = lax.broadcasted_iota(jnp.int32, (devices, 128), 0)
    lags = []
    for i in range(nv):
        lag = jnp.zeros((devices, 128), F32)
        for d in range(devices):
            gap = (length - 1 + d * length - pos_ref[d * nv + i]).astype(F32)
            lag = jnp.where(row == d, gap, lag)
        lags.append(lag)
    combine(nv, length, lags, got_ref, rate_ref[:, mine], residue_ref[:, mine], back_ref)
    second_leg = hand_out(back_ref, enter_ref, own_sems.at[1], send_sems.at[1], recv_sems.at[1])
    lax.fori_loop(early, chunks, local, 0)
    for copy in second_leg:
        copy.wait()

    def finish(j, carry):
        cols = columns(j)
        q = rows_ref[0, :, cols].astype(F32)
        entering = jnp.concatenate(
            [
                enter_ref[j * owners + d, c * 2 * KD : (c + 1) * 2 * KD, :]
                for d in range(owners)
                for c in range(tiles)
            ],
            axis=1,
        )
        zeros = jnp.zeros((16 - KD, chunk), F32)
        z = jnp.concatenate([entering[:KD], zeros], axis=0)
        inner = inner_ref[:, cols] + jnp.dot(gd_ref[...], split3_rhs(z), preferred_element_type=F32)
        out_ref[:, cols] = (q * inner).astype(out_ref.dtype)
        z = jnp.concatenate([entering[KD:], zeros], axis=0)
        delta = delta_ref[:, cols] + jnp.dot(gd_ref[...], split3_rhs(z), preferred_element_type=F32)
        table = base_ref[0, :, cols].astype(F32)
        total = jnp.zeros((1, chunk), F32)
        for i in range(nv):
            new = jnp.sum(jnp.where(pick == alts[i], table, 0.0), axis=0, keepdims=True)
            gate = q[slabs[i]]
            gate_step = jnp.where(step == places[i], new - gate, 0.0)
            change = (gate + gate_step) * delta[slabs[i]] + gate_step * inner[slabs[i]]
            effect_ref[slabs[i], cols] = change.astype(effect_ref.dtype)
            total = total + jnp.sum(change, axis=0, keepdims=True)
        for d in range(owners):
            for c in range(tiles):
                lanes = (d * tiles + c) * 128
                parts_ref[j * owners + d, c : c + 1, :] = total[:, lanes : lanes + 128]
        return carry

    lax.fori_loop(0, chunks, finish, 0)
    for copy in hand_out(parts_ref, sums_ref, own_sems.at[2], send_sems.at[2], recv_sems.at[2]):
        copy.wait()
    score_ref[...] = jnp.sum(sums_ref[...], axis=0)


def on_device(features, base_rows, positions, alt_bases, decay_rate, residue, skip_gain):
    length, _, width = features.shape
    devices = lax.axis_size("context")
    nv = positions.shape[0] // devices
    share = width // devices
    tiles = share // 128
    half = length // 2
    table = cheb_table(length)

    gm = jnp.asarray(split3_lhs(pad_rows(table[::-1, :KD].T, 16)))
    lag = np.arange(half)[:, None] - np.arange(half)[None]
    toeplitz = np.where((lag >= 0)[None], table[np.maximum(lag, 0), :KB].transpose(2, 0, 1), 0.0)
    toeplitz = toeplitz.reshape(KB * half, half)
    ends = pad_rows(table[:half, :KB][::-1].T, 8)
    gb = jnp.asarray(split3_lhs(np.concatenate([toeplitz, ends], axis=0)))
    gx = jnp.asarray(split3_lhs(pad_cols(table[:half, :KB], 16)))
    gd = jnp.asarray(split3_lhs(pad_cols(table[:, :KD], 16)))

    smem = pl.BlockSpec(memory_space=pltpu.SMEM)
    vmem = pl.BlockSpec(memory_space=pltpu.VMEM)
    ref_out, effect, channel_score = pl.pallas_call(
        functools.partial(kernel, nv),
        in_specs=[smem, smem] + [vmem] * 9,
        out_specs=[vmem] * 3,
        out_shape=[
            jax.ShapeDtypeStruct((length, width), BF16),
            jax.ShapeDtypeStruct((length, width), BF16),
            jax.ShapeDtypeStruct((tiles, 128), F32),
        ],
        scratch_shapes=[
            pltpu.VMEM((devices, tiles * (KD + nv), 128), F32),
            pltpu.VMEM((devices, tiles * (KD + nv), 128), F32),
            pltpu.VMEM((devices, tiles * 2 * KD, 128), F32),
            pltpu.VMEM((devices, tiles * 2 * KD, 128), F32),
            pltpu.VMEM((length, width), F32),
            pltpu.VMEM((length, width), F32),
            pltpu.VMEM((4, 2 * length, 128), F32),
            pltpu.VMEM((devices, tiles, 128), F32),
            pltpu.VMEM((devices, tiles, 128), F32),
            pltpu.SemaphoreType.DMA((3,)),
            pltpu.SemaphoreType.DMA((3, devices)),
            pltpu.SemaphoreType.DMA((3, devices)),
        ],
        compiler_params=pltpu.CompilerParams(collective_id=0, has_side_effects=True),
        name="score_variants",
    )(
        positions, alt_bases, gm, gb, gx, gd, features.transpose(1, 0, 2), base_rows.transpose(1, 0, 2),
        decay_rate, residue, skip_gain.reshape(1, width),
    )
    return ref_out, effect, channel_score.reshape(share)


def solution(mesh):
    return jax.shard_map(
        on_device,
        mesh=mesh,
        in_specs=(P(("group", "context"), None, None), P(), P("group"), P("group"), P(), P(), P()),
        out_specs=(
            P(("group", "context"), None),
            P(("group", "context"), None),
            P(("group", "context")),
        ),
        check_vma=False,
    )
```

```python
import functools

import jax
import jax.numpy as jnp
import numpy as np
from jax import lax
from jax.experimental import pallas as pl
from jax.experimental.pallas import tpu as pltpu
from jax.sharding import PartitionSpec as P

F32 = jnp.float32
BF16 = jnp.bfloat16
MESH = pl.DeviceIdType.MESH
RATE_MAX = 0.03
KD = 10
KF = 6
KB = 7


def cheb_table(length):
    nodes = 64
    theta = (np.arange(nodes) + 0.5) * np.pi / nodes
    rate = (np.cos(theta) + 1.0) * (RATE_MAX / 2)
    values = np.exp(-rate[None] * np.arange(length)[:, None])
    basis = np.cos(np.arange(16)[:, None] * theta[None])
    table = 2.0 / nodes * values @ basis.T
    table[:, 0] *= 0.5
    return table


def split3_lhs(a):
    a = a.astype(np.float32)
    hi = a.astype(jnp.bfloat16)
    lo = (a - hi.astype(np.float32)).astype(jnp.bfloat16)
    return np.concatenate([hi, lo, hi], axis=1)


def split3_rhs(x):
    hi = x.astype(BF16)
    lo = (x - hi.astype(F32)).astype(BF16)
    return jnp.concatenate([hi, hi, lo], axis=0)


def pad_rows(a, rows):
    return np.concatenate([a, np.zeros((rows - a.shape[0],) + a.shape[1:])], axis=0)


def pad_cols(a, cols):
    return np.concatenate([a, np.zeros((a.shape[0], cols - a.shape[1]))], axis=1)


def cheb_terms(rate, count):
    x = rate * (2.0 / RATE_MAX) - 1.0
    terms = [jnp.ones_like(x), x]
    while len(terms) < count:
        terms.append(2.0 * x * terms[-1] - terms[-2])
    return terms


def modal_coef(rate, residue):
    z = 2.0 * rate
    tail = 1.0 - z * (1.0 / 2) * (1.0 - z * (1.0 / 3) * (1.0 - z * (1.0 / 4) * (1.0 - z * (1.0 / 5) * (1.0 - z * (1.0 / 6)))))
    return residue * jnp.sqrt(z * tail)


def combine(nv, length, lags, in_ref, low_ref, my_rate, my_residue, out_ref, out_low_ref, part):
    devices = in_ref.shape[0]
    height = KF + nv
    small = KD - KF
    row = lax.broadcasted_iota(jnp.int32, (devices, 128), 0)

    def before(ends, rate_n):
        ends = jnp.where(row >= 1, pltpu.roll(ends, 1, 0), 0.0)
        hop = 1
        while hop < devices:
            fade = jnp.exp(rate_n * (-float(length) * hop))
            ends = ends + fade * jnp.where(row >= hop, pltpu.roll(ends, hop, 0), 0.0)
            hop *= 2
        return ends

    for c in part:
        rate = my_rate[:, c * 128 : (c + 1) * 128]
        terms = cheb_terms(rate, KD)
        lead = modal_coef(rate, my_residue[:, c * 128 : (c + 1) * 128]) * jnp.exp(-rate)
        leads = [lead * term for term in terms]
        moments = [in_ref[:, c * height + k, :] for k in range(KF)]
        moments += [low_ref[:, c * small + k, :] for k in range(small)]
        subs = [in_ref[:, c * height + KF + i, :] for i in range(nv)]
        base = [jnp.zeros((devices, 128), F32) for _ in range(KD)]
        change = [jnp.zeros((devices, 128), F32) for _ in range(KD)]
        for n in range(rate.shape[0]):
            rate_n = rate[n : n + 1]
            ends = terms[0][n : n + 1] * moments[0]
            for k in range(1, KD):
                ends = ends + terms[k][n : n + 1] * moments[k]
            shifted = jnp.exp(-rate_n * lags[0]) * subs[0]
            for i in range(1, nv):
                shifted = shifted + jnp.exp(-rate_n * lags[i]) * subs[i]
            ends, shifted = before(ends, rate_n), before(shifted, rate_n)
            for k in range(KD):
                base[k] = base[k] + leads[k][n : n + 1] * ends
                change[k] = change[k] + leads[k][n : n + 1] * shifted
        for k in range(KF):
            out_ref[:, c * 2 * KF + k, :] = base[k]
            out_ref[:, c * 2 * KF + KF + k, :] = change[k]
        for k in range(small):
            out_low_ref[:, c * 2 * small + k, :] = base[KF + k]
            out_low_ref[:, c * 2 * small + small + k, :] = change[KF + k]


def greet(devices):
    me = lax.axis_index("context")
    barrier = pltpu.get_barrier_semaphore()
    for hop in range(1, devices):
        pl.semaphore_signal(
            barrier, inc=1, device_id={"context": lax.rem(me + hop, devices)}, device_id_type=MESH
        )
    return lambda: pl.semaphore_wait(barrier, devices - 1)


def hand_out(src_ref, dst_ref, send_sems, recv_sems, leg, hops=None, first=0, count=None):
    devices = src_ref.shape[0]
    me = lax.axis_index("context")
    rows = pl.ds(first, src_ref.shape[1] if count is None else count)
    copies = []
    for hop in range(devices) if hops is None else hops:
        if hop == 0:
            copies.append(pltpu.make_async_copy(src_ref.at[me, rows], dst_ref.at[me, rows], send_sems.at[leg, 0]))
        else:
            peer = lax.rem(me + hop, devices)
            copies.append(
                pltpu.make_async_remote_copy(
                    src_ref=src_ref.at[peer, rows],
                    dst_ref=dst_ref.at[me, rows],
                    send_sem=send_sems.at[leg, hop],
                    recv_sem=recv_sems.at[leg, hop],
                    device_id={"context": peer},
                    device_id_type=MESH,
                )
            )
        copies[-1].start()
    return copies


def kernel(
    nv, pos_ref, alt_ref, gm_ref, gb_ref, gx_ref, gd_ref, rows_ref, base_ref, rate_ref, residue_ref, skip_ref,
    out_ref, effect_ref, score_ref,
    mine_ref, got_ref, back_ref, enter_ref, mine_low_ref, got_low_ref, back_low_ref, enter_low_ref,
    low_in_ref, low_out_ref, inner_ref, delta_ref, pad_ref, parts_ref, sums_ref, send_sems, recv_sems,
):
    length, width = out_ref.shape
    devices, me = lax.axis_size("context"), lax.axis_index("context")
    share = width // devices
    tiles = share // 128
    half, stretch = length // 2, length // nv
    chunk = 512
    chunks, owners = width // chunk, chunk // share
    small = KD - KF
    step = lax.broadcasted_iota(jnp.int32, (stretch, 1), 0)
    pick = lax.broadcasted_iota(jnp.int32, (base_ref.shape[1], 1), 0)
    places = [lax.rem(pos_ref[me * nv + i], stretch) for i in range(nv)]
    alts = [alt_ref[me * nv + i] for i in range(nv)]
    slabs = [slice(i * stretch, (i + 1) * stretch) for i in range(nv)]

    def columns(j):
        return pl.ds(pl.multiple_of(j * chunk, chunk), chunk)

    def force(cols):
        return rows_ref[1, :, cols].astype(F32) * rows_ref[2, :, cols].astype(F32)

    def force_steps(forcing, cols):
        table = base_ref[1, :, cols].astype(F32) * base_ref[2, :, cols].astype(F32)
        steps = []
        for i in range(nv):
            new = jnp.sum(jnp.where(pick == alts[i], table, 0.0), axis=0, keepdims=True)
            steps.append(jnp.where(step == places[i], new - forcing[slabs[i]], 0.0))
        return steps

    barrier_wait = greet(devices)

    def moments(j, carry):
        j = lax.rem(me // owners + j, chunks)
        cols = columns(j)
        forcing = force(cols)
        sums = jnp.dot(gm_ref[...], split3_rhs(forcing), preferred_element_type=F32)
        steps = [jnp.sum(part, axis=0, keepdims=True) for part in force_steps(forcing, cols)]
        packed = jnp.concatenate([sums[:KF]] + steps, axis=0)
        for d in range(owners):
            low = []
            for c in range(tiles):
                lanes = (d * tiles + c) * 128
                mine_ref[j * owners + d, c * (KF + nv) : (c + 1) * (KF + nv), :] = packed[:, lanes : lanes + 128]
                low.append(sums[KF:KD, lanes : lanes + 128])
            mine_low_ref[j * owners + d] = jnp.concatenate(low, axis=0).astype(BF16)
        return carry

    lax.fori_loop(0, chunks // 2, moments, 0)
    barrier_wait()
    near = range(1, devices // 2 - owners + 1)
    rest = [hop for hop in range(devices) if hop not in near]
    first_leg = hand_out(mine_ref, got_ref, send_sems, recv_sems, 0, near)
    first_leg += hand_out(mine_low_ref, got_low_ref, send_sems, recv_sems, 1, near)
    lax.fori_loop(chunks // 2, chunks, moments, 0)
    first_leg += hand_out(mine_ref, got_ref, send_sems, recv_sems, 0, rest)
    first_leg += hand_out(mine_low_ref, got_low_ref, send_sems, recv_sems, 1, rest)

    def local(j, carry):
        cols = columns(j)
        forcing = force(cols)
        skip = skip_ref[:, cols]
        rate = rate_ref[:, cols]
        terms = cheb_terms(rate, KD)
        coef = modal_coef(rate, residue_ref[:, cols])
        lead = coef * jnp.exp(-rate)
        weights = [jnp.sum(coef * term, axis=0, keepdims=True) for term in terms]
        filtered = []
        for b in range(2):
            products = jnp.dot(
                gb_ref[...], split3_rhs(forcing[b * half : (b + 1) * half]), preferred_element_type=F32
            )
            total = weights[0] * products[:half]
            for k in range(1, KB):
                total = total + weights[k] * products[k * half : (k + 1) * half]
            filtered.append(total)
            if b == 0:
                first = products[KB * half : KB * half + KB]
        state = terms[0] * first[0:1]
        for k in range(1, KB):
            state = state + terms[k] * first[k : k + 1]
        state = lead * state
        zeros = jnp.zeros((16, chunk), F32)
        cross = [jnp.sum(terms[k] * state, axis=0, keepdims=True) for k in range(KB)]
        z = jnp.concatenate(cross + [zeros[: 16 - KB]], axis=0)
        filtered[1] = filtered[1] + jnp.dot(gx_ref[...], split3_rhs(z), preferred_element_type=F32)
        inner_ref[:, cols] = jnp.concatenate(filtered, axis=0) + skip * forcing

        z = jnp.concatenate(weights + [zeros[: 16 - KD]], axis=0)
        impulse = jnp.dot(gd_ref[...], split3_rhs(z), preferred_element_type=F32)
        for c in range(chunk // 128):
            pad_ref[c, length:, :] = impulse[:, c * 128 : (c + 1) * 128]
        steps = force_steps(forcing, cols)
        deltas = [skip * part for part in steps]
        for i in range(nv):
            impact = jnp.sum(steps[i], axis=0, keepdims=True)
            for j2 in range(i, nv):
                response = jnp.concatenate(
                    [
                        pad_ref[c, pl.ds(length + (j2 - i) * stretch - places[i], stretch), :]
                        for c in range(chunk // 128)
                    ],
                    axis=1,
                )
                deltas[j2] = deltas[j2] + response * impact
        for i in range(nv):
            delta_ref[slabs[i], cols] = deltas[i]
        return carry

    for c in range(chunk // 128):
        pad_ref[c, :length, :] = jnp.zeros((length, 128), F32)
    early = chunks // 2
    lax.fori_loop(0, early, local, 0)

    for copy in first_leg:
        copy.wait()
    mine = pl.ds(pl.multiple_of(me * share, share), share)
    row = lax.broadcasted_iota(jnp.int32, (devices, 128), 0)
    lags = []
    for i in range(nv):
        lag = jnp.zeros((devices, 128), F32)
        for d in range(devices):
            gap = (length - 1 + d * length - pos_ref[d * nv + i]).astype(F32)
            lag = jnp.where(row == d, gap, lag)
        lags.append(lag)
    low_in_ref[...] = got_low_ref[...].astype(F32)
    pieces = 2 if tiles > 1 else 1
    span = tiles // pieces
    second_leg = []
    for p in range(pieces):
        combine(
            nv, length, lags, got_ref, low_in_ref, rate_ref[:, mine], residue_ref[:, mine], back_ref, low_out_ref,
            range(p * span, (p + 1) * span),
        )
        first, count = p * span * 2 * small, span * 2 * small
        back_low_ref[:, first : first + count, :] = low_out_ref[:, first : first + count, :].astype(BF16)
        second_leg += hand_out(
            back_ref, enter_ref, send_sems, recv_sems, 2 + p, None, p * span * 2 * KF, span * 2 * KF
        )
        second_leg += hand_out(back_low_ref, enter_low_ref, send_sems, recv_sems, 4 + p, None, first, count)
    lax.fori_loop(early, chunks, local, 0)
    for copy in second_leg:
        copy.wait()

    def finish(j, carry):
        cols = columns(j)
        q = rows_ref[0, :, cols].astype(F32)
        lead, tail = [], []
        for d in range(owners):
            low = enter_low_ref[j * owners + d].astype(F32)
            for c in range(tiles):
                lead.append(enter_ref[j * owners + d, c * 2 * KF : (c + 1) * 2 * KF, :])
                tail.append(low[c * 2 * small : (c + 1) * 2 * small])
        lead, tail = jnp.concatenate(lead, axis=1), jnp.concatenate(tail, axis=1)
        zeros = jnp.zeros((16 - KD, chunk), F32)
        z = jnp.concatenate([lead[:KF], tail[:small], zeros], axis=0)
        inner = inner_ref[:, cols] + jnp.dot(gd_ref[...], split3_rhs(z), preferred_element_type=F32)
        out_ref[:, cols] = (q * inner).astype(out_ref.dtype)
        z = jnp.concatenate([lead[KF:], tail[small:], zeros], axis=0)
        delta = delta_ref[:, cols] + jnp.dot(gd_ref[...], split3_rhs(z), preferred_element_type=F32)
        table = base_ref[0, :, cols].astype(F32)
        total = jnp.zeros((1, chunk), F32)
        for i in range(nv):
            new = jnp.sum(jnp.where(pick == alts[i], table, 0.0), axis=0, keepdims=True)
            gate = q[slabs[i]]
            gate_step = jnp.where(step == places[i], new - gate, 0.0)
            change = (gate + gate_step) * delta[slabs[i]] + gate_step * inner[slabs[i]]
            effect_ref[slabs[i], cols] = change.astype(effect_ref.dtype)
            total = total + jnp.sum(change, axis=0, keepdims=True)
        for d in range(owners):
            for c in range(tiles):
                lanes = (d * tiles + c) * 128
                parts_ref[j * owners + d, c : c + 1, :] = total[:, lanes : lanes + 128]
        return carry

    lax.fori_loop(0, chunks, finish, 0)
    for copy in hand_out(parts_ref, sums_ref, send_sems, recv_sems, 6):
        copy.wait()
    score_ref[...] = jnp.sum(sums_ref[...], axis=0)


def on_device(features, base_rows, positions, alt_bases, decay_rate, residue, skip_gain):
    length, _, width = features.shape
    devices = lax.axis_size("context")
    nv = positions.shape[0] // devices
    share = width // devices
    tiles = share // 128
    half = length // 2
    table = cheb_table(length)

    gm = jnp.asarray(split3_lhs(pad_rows(table[::-1, :KD].T, 16)))
    lag = np.arange(half)[:, None] - np.arange(half)[None]
    toeplitz = np.where((lag >= 0)[None], table[np.maximum(lag, 0), :KB].transpose(2, 0, 1), 0.0)
    toeplitz = toeplitz.reshape(KB * half, half)
    ends = pad_rows(table[:half, :KB][::-1].T, 8)
    gb = jnp.asarray(split3_lhs(np.concatenate([toeplitz, ends], axis=0)))
    gx = jnp.asarray(split3_lhs(pad_cols(table[:half, :KB], 16)))
    gd = jnp.asarray(split3_lhs(pad_cols(table[:, :KD], 16)))

    smem = pl.BlockSpec(memory_space=pltpu.SMEM)
    vmem = pl.BlockSpec(memory_space=pltpu.VMEM)
    ref_out, effect, channel_score = pl.pallas_call(
        functools.partial(kernel, nv),
        in_specs=[smem, smem] + [vmem] * 9,
        out_specs=[vmem] * 3,
        out_shape=[
            jax.ShapeDtypeStruct((length, width), BF16),
            jax.ShapeDtypeStruct((length, width), BF16),
            jax.ShapeDtypeStruct((tiles, 128), F32),
        ],
        scratch_shapes=[
            pltpu.VMEM((devices, tiles * (KF + nv), 128), F32),
            pltpu.VMEM((devices, tiles * (KF + nv), 128), F32),
            pltpu.VMEM((devices, tiles * 2 * KF, 128), F32),
            pltpu.VMEM((devices, tiles * 2 * KF, 128), F32),
            pltpu.VMEM((devices, tiles * (KD - KF), 128), BF16),
            pltpu.VMEM((devices, tiles * (KD - KF), 128), BF16),
            pltpu.VMEM((devices, tiles * 2 * (KD - KF), 128), BF16),
            pltpu.VMEM((devices, tiles * 2 * (KD - KF), 128), BF16),
            pltpu.VMEM((devices, tiles * (KD - KF), 128), F32),
            pltpu.VMEM((devices, tiles * 2 * (KD - KF), 128), F32),
            pltpu.VMEM((length, width), F32),
            pltpu.VMEM((length, width), F32),
            pltpu.VMEM((4, 2 * length, 128), F32),
            pltpu.VMEM((devices, tiles, 128), F32),
            pltpu.VMEM((devices, tiles, 128), F32),
            pltpu.SemaphoreType.DMA((7, devices)),
            pltpu.SemaphoreType.DMA((7, devices)),
        ],
        compiler_params=pltpu.CompilerParams(
            collective_id=0, has_side_effects=True, vmem_limit_bytes=36 << 20
        ),
        name="score_variants",
    )(
        positions, alt_bases, gm, gb, gx, gd, features.transpose(1, 0, 2), base_rows.transpose(1, 0, 2),
        decay_rate, residue, skip_gain.reshape(1, width),
    )
    return ref_out, effect, channel_score.reshape(share)


def solution(mesh):
    return jax.shard_map(
        on_device,
        mesh=mesh,
        in_specs=(P(("group", "context"), None, None), P(), P("group"), P("group"), P(), P(), P()),
        out_specs=(
            P(("group", "context"), None),
            P(("group", "context"), None),
            P(("group", "context")),
        ),
        check_vma=False,
    )
```

```python
import functools

import jax
import jax.numpy as jnp
import numpy as np
from jax import lax
from jax.experimental import pallas as pl
from jax.experimental.pallas import tpu as pltpu
from jax.sharding import PartitionSpec as P

F32 = jnp.float32
BF16 = jnp.bfloat16
MESH = pl.DeviceIdType.MESH
RATE_MAX = 0.03
KD = 10
KF = 6
KB = 7


def cheb_table(length):
    nodes = 64
    theta = (np.arange(nodes) + 0.5) * np.pi / nodes
    rate = (np.cos(theta) + 1.0) * (RATE_MAX / 2)
    values = np.exp(-rate[None] * np.arange(length)[:, None])
    basis = np.cos(np.arange(16)[:, None] * theta[None])
    table = 2.0 / nodes * values @ basis.T
    table[:, 0] *= 0.5
    return table


def split3_lhs(a):
    a = a.astype(np.float32)
    hi = a.astype(jnp.bfloat16)
    lo = (a - hi.astype(np.float32)).astype(jnp.bfloat16)
    return np.concatenate([hi, lo, hi], axis=1)


def split3_rhs(x):
    hi = x.astype(BF16)
    lo = (x - hi.astype(F32)).astype(BF16)
    return jnp.concatenate([hi, hi, lo], axis=0)


def pad_rows(a, rows):
    return np.concatenate([a, np.zeros((rows - a.shape[0],) + a.shape[1:])], axis=0)


def pad_cols(a, cols):
    return np.concatenate([a, np.zeros((a.shape[0], cols - a.shape[1]))], axis=1)


def cheb_terms(rate, count):
    x = rate * (2.0 / RATE_MAX) - 1.0
    terms = [jnp.ones_like(x), x]
    while len(terms) < count:
        terms.append(2.0 * x * terms[-1] - terms[-2])
    return terms


def modal_coef(rate, residue):
    z = 2.0 * rate
    tail = 1.0 - z * (1.0 / 2) * (1.0 - z * (1.0 / 3) * (1.0 - z * (1.0 / 4) * (1.0 - z * (1.0 / 5) * (1.0 - z * (1.0 / 6)))))
    return residue * jnp.sqrt(z * tail)


def combine(nv, length, lags, in_ref, low_ref, my_rate, my_residue, out_ref, out_low_ref, part):
    devices = in_ref.shape[0]
    height = KF + nv
    small = KD - KF
    row = lax.broadcasted_iota(jnp.int32, (devices, 128), 0)

    def before(ends, rate_n):
        ends = jnp.where(row >= 1, pltpu.roll(ends, 1, 0), 0.0)
        hop = 1
        while hop < devices:
            fade = jnp.exp(rate_n * (-float(length) * hop))
            ends = ends + fade * jnp.where(row >= hop, pltpu.roll(ends, hop, 0), 0.0)
            hop *= 2
        return ends

    for c in part:
        rate = my_rate[:, c * 128 : (c + 1) * 128]
        terms = cheb_terms(rate, KD)
        lead = modal_coef(rate, my_residue[:, c * 128 : (c + 1) * 128]) * jnp.exp(-rate)
        leads = [lead * term for term in terms]
        moments = [in_ref[:, c * height + k, :] for k in range(KF)]
        moments += [low_ref[:, c * small + k, :] for k in range(small)]
        subs = [in_ref[:, c * height + KF + i, :] for i in range(nv)]
        base = [jnp.zeros((devices, 128), F32) for _ in range(KD)]
        change = [jnp.zeros((devices, 128), F32) for _ in range(KD)]
        for n in range(rate.shape[0]):
            rate_n = rate[n : n + 1]
            ends = terms[0][n : n + 1] * moments[0]
            for k in range(1, KD):
                ends = ends + terms[k][n : n + 1] * moments[k]
            shifted = jnp.exp(-rate_n * lags[0]) * subs[0]
            for i in range(1, nv):
                shifted = shifted + jnp.exp(-rate_n * lags[i]) * subs[i]
            ends, shifted = before(ends, rate_n), before(shifted, rate_n)
            for k in range(KD):
                base[k] = base[k] + leads[k][n : n + 1] * ends
                change[k] = change[k] + leads[k][n : n + 1] * shifted
        for k in range(KF):
            out_ref[:, c * 2 * KF + k, :] = base[k]
            out_ref[:, c * 2 * KF + KF + k, :] = change[k]
        for k in range(small):
            out_low_ref[:, c * 2 * small + k, :] = base[KF + k]
            out_low_ref[:, c * 2 * small + small + k, :] = change[KF + k]


def greet(devices):
    me = lax.axis_index("context")
    barrier = pltpu.get_barrier_semaphore()
    for hop in range(1, devices):
        pl.semaphore_signal(
            barrier, inc=1, device_id={"context": lax.rem(me + hop, devices)}, device_id_type=MESH
        )
    return lambda: pl.semaphore_wait(barrier, devices - 1)


def hand_out(src_ref, dst_ref, send_sems, recv_sems, leg, hops=None, first=0, count=None):
    devices = src_ref.shape[0]
    me = lax.axis_index("context")
    rows = pl.ds(first, src_ref.shape[1] if count is None else count)
    copies = []
    for hop in range(devices) if hops is None else hops:
        if hop == 0:
            copies.append(pltpu.make_async_copy(src_ref.at[me, rows], dst_ref.at[me, rows], send_sems.at[leg, 0]))
        else:
            peer = lax.rem(me + hop, devices)
            copies.append(
                pltpu.make_async_remote_copy(
                    src_ref=src_ref.at[peer, rows],
                    dst_ref=dst_ref.at[me, rows],
                    send_sem=send_sems.at[leg, hop],
                    recv_sem=recv_sems.at[leg, hop],
                    device_id={"context": peer},
                    device_id_type=MESH,
                )
            )
        copies[-1].start()
    return copies


def kernel(
    nv, pos_in, alt_in, gm_in, gb_in, gx_in, gd_in, rows_in, base_in, rate_in, residue_in, skip_in,
    out_hbm, effect_hbm, score_ref,
    out_ref, effect_ref, pos_ref, alt_ref, gm_ref, gb_ref, gx_ref, gd_ref, rows_ref, base_ref, rate_ref, residue_ref, skip_ref, load_sems,
    mine_ref, got_ref, back_ref, enter_ref, mine_low_ref, got_low_ref, back_low_ref, enter_low_ref,
    low_in_ref, low_out_ref, inner_ref, delta_ref, pad_ref, parts_ref, sums_ref, send_sems, recv_sems,
):
    length, width = out_ref.shape
    devices, me = lax.axis_size("context"), lax.axis_index("context")
    share = width // devices
    tiles = share // 128
    half, stretch = length // 2, length // nv
    chunk = 512
    chunks, owners = width // chunk, chunk // share
    small = KD - KF
    loads = [
        (pos_in, pos_ref), (alt_in, alt_ref), (base_in, base_ref), (gm_in, gm_ref),
        (rows_in.at[1], rows_ref.at[1]), (rows_in.at[2], rows_ref.at[2]), (gb_in, gb_ref), (gx_in, gx_ref),
        (gd_in, gd_ref), (rate_in, rate_ref), (residue_in, residue_ref), (skip_in, skip_ref),
        (rows_in.at[0], rows_ref.at[0]),
    ]
    loads = [pltpu.make_async_copy(src, dst, load_sems.at[i]) for i, (src, dst) in enumerate(loads)]
    for load in loads:
        load.start()
    barrier_wait = greet(devices)
    for load in loads[:6]:
        load.wait()
    step = lax.broadcasted_iota(jnp.int32, (stretch, 1), 0)
    pick = lax.broadcasted_iota(jnp.int32, (base_ref.shape[1], 1), 0)
    places = [lax.rem(pos_ref[me * nv + i], stretch) for i in range(nv)]
    alts = [alt_ref[me * nv + i] for i in range(nv)]
    slabs = [slice(i * stretch, (i + 1) * stretch) for i in range(nv)]

    def columns(j):
        return pl.ds(pl.multiple_of(j * chunk, chunk), chunk)

    def force(cols):
        return rows_ref[1, :, cols].astype(F32) * rows_ref[2, :, cols].astype(F32)

    def force_steps(forcing, cols):
        table = base_ref[1, :, cols].astype(F32) * base_ref[2, :, cols].astype(F32)
        steps = []
        for i in range(nv):
            new = jnp.sum(jnp.where(pick == alts[i], table, 0.0), axis=0, keepdims=True)
            steps.append(jnp.where(step == places[i], new - forcing[slabs[i]], 0.0))
        return steps

    def moments(j, carry):
        j = lax.rem(me // owners + j, chunks)
        cols = columns(j)
        forcing = force(cols)
        sums = jnp.dot(gm_ref[...], split3_rhs(forcing), preferred_element_type=F32)
        steps = [jnp.sum(part, axis=0, keepdims=True) for part in force_steps(forcing, cols)]
        packed = jnp.concatenate([sums[:KF]] + steps, axis=0)
        for d in range(owners):
            low = []
            for c in range(tiles):
                lanes = (d * tiles + c) * 128
                mine_ref[j * owners + d, c * (KF + nv) : (c + 1) * (KF + nv), :] = packed[:, lanes : lanes + 128]
                low.append(sums[KF:KD, lanes : lanes + 128])
            mine_low_ref[j * owners + d] = jnp.concatenate(low, axis=0).astype(BF16)
        return carry

    lax.fori_loop(0, chunks // 2, moments, 0)
    barrier_wait()
    near = range(1, devices // 2 - owners + 1)
    rest = [hop for hop in range(devices) if hop not in near]
    first_leg = hand_out(mine_ref, got_ref, send_sems, recv_sems, 0, near)
    first_leg += hand_out(mine_low_ref, got_low_ref, send_sems, recv_sems, 1, near)
    lax.fori_loop(chunks // 2, chunks, moments, 0)
    first_leg += hand_out(mine_ref, got_ref, send_sems, recv_sems, 0, rest)
    first_leg += hand_out(mine_low_ref, got_low_ref, send_sems, recv_sems, 1, rest)

    def local(j, carry):
        cols = columns(j)
        forcing = force(cols)
        skip = skip_ref[:, cols]
        rate = rate_ref[:, cols]
        terms = cheb_terms(rate, KD)
        coef = modal_coef(rate, residue_ref[:, cols])
        lead = coef * jnp.exp(-rate)
        weights = [jnp.sum(coef * term, axis=0, keepdims=True) for term in terms]
        filtered = []
        for b in range(2):
            products = jnp.dot(
                gb_ref[...], split3_rhs(forcing[b * half : (b + 1) * half]), preferred_element_type=F32
            )
            total = weights[0] * products[:half]
            for k in range(1, KB):
                total = total + weights[k] * products[k * half : (k + 1) * half]
            filtered.append(total)
            if b == 0:
                first = products[KB * half : KB * half + KB]
        state = terms[0] * first[0:1]
        for k in range(1, KB):
            state = state + terms[k] * first[k : k + 1]
        state = lead * state
        zeros = jnp.zeros((16, chunk), F32)
        cross = [jnp.sum(terms[k] * state, axis=0, keepdims=True) for k in range(KB)]
        z = jnp.concatenate(cross + [zeros[: 16 - KB]], axis=0)
        filtered[1] = filtered[1] + jnp.dot(gx_ref[...], split3_rhs(z), preferred_element_type=F32)
        inner_ref[:, cols] = jnp.concatenate(filtered, axis=0) + skip * forcing

        z = jnp.concatenate(weights + [zeros[: 16 - KD]], axis=0)
        impulse = jnp.dot(gd_ref[...], split3_rhs(z), preferred_element_type=F32)
        for c in range(chunk // 128):
            pad_ref[c, length:, :] = impulse[:, c * 128 : (c + 1) * 128]
        steps = force_steps(forcing, cols)
        deltas = [skip * part for part in steps]
        for i in range(nv):
            impact = jnp.sum(steps[i], axis=0, keepdims=True)
            for j2 in range(i, nv):
                response = jnp.concatenate(
                    [
                        pad_ref[c, pl.ds(length + (j2 - i) * stretch - places[i], stretch), :]
                        for c in range(chunk // 128)
                    ],
                    axis=1,
                )
                deltas[j2] = deltas[j2] + response * impact
        for i in range(nv):
            delta_ref[slabs[i], cols] = deltas[i]
        return carry

    for c in range(chunk // 128):
        pad_ref[c, :length, :] = jnp.zeros((length, 128), F32)
    early = chunks // 2
    for load in loads[6:]:
        load.wait()
    lax.fori_loop(0, early, local, 0)

    for copy in first_leg:
        copy.wait()
    mine = pl.ds(pl.multiple_of(me * share, share), share)
    row = lax.broadcasted_iota(jnp.int32, (devices, 128), 0)
    lags = []
    for i in range(nv):
        lag = jnp.zeros((devices, 128), F32)
        for d in range(devices):
            gap = (length - 1 + d * length - pos_ref[d * nv + i]).astype(F32)
            lag = jnp.where(row == d, gap, lag)
        lags.append(lag)
    low_in_ref[...] = got_low_ref[...].astype(F32)
    pieces = 2 if tiles > 1 else 1
    span = tiles // pieces
    second_leg = []
    for p in range(pieces):
        combine(
            nv, length, lags, got_ref, low_in_ref, rate_ref[:, mine], residue_ref[:, mine], back_ref, low_out_ref,
            range(p * span, (p + 1) * span),
        )
        first, count = p * span * 2 * small, span * 2 * small
        back_low_ref[:, first : first + count, :] = low_out_ref[:, first : first + count, :].astype(BF16)
        second_leg += hand_out(
            back_ref, enter_ref, send_sems, recv_sems, 2 + p, None, p * span * 2 * KF, span * 2 * KF
        )
        second_leg += hand_out(back_low_ref, enter_low_ref, send_sems, recv_sems, 4 + p, None, first, count)
    lax.fori_loop(early, chunks, local, 0)
    for copy in second_leg:
        copy.wait()

    def finish(j, carry):
        cols = columns(j)
        q = rows_ref[0, :, cols].astype(F32)
        lead, tail = [], []
        for d in range(owners):
            low = enter_low_ref[j * owners + d].astype(F32)
            for c in range(tiles):
                lead.append(enter_ref[j * owners + d, c * 2 * KF : (c + 1) * 2 * KF, :])
                tail.append(low[c * 2 * small : (c + 1) * 2 * small])
        lead, tail = jnp.concatenate(lead, axis=1), jnp.concatenate(tail, axis=1)
        zeros = jnp.zeros((16 - KD, chunk), F32)
        z = jnp.concatenate([lead[:KF], tail[:small], zeros], axis=0)
        inner = inner_ref[:, cols] + jnp.dot(gd_ref[...], split3_rhs(z), preferred_element_type=F32)
        out_ref[:, cols] = (q * inner).astype(out_ref.dtype)
        z = jnp.concatenate([lead[KF:], tail[small:], zeros], axis=0)
        delta = delta_ref[:, cols] + jnp.dot(gd_ref[...], split3_rhs(z), preferred_element_type=F32)
        table = base_ref[0, :, cols].astype(F32)
        total = jnp.zeros((1, chunk), F32)
        for i in range(nv):
            new = jnp.sum(jnp.where(pick == alts[i], table, 0.0), axis=0, keepdims=True)
            gate = q[slabs[i]]
            gate_step = jnp.where(step == places[i], new - gate, 0.0)
            change = (gate + gate_step) * delta[slabs[i]] + gate_step * inner[slabs[i]]
            effect_ref[slabs[i], cols] = change.astype(effect_ref.dtype)
            total = total + jnp.sum(change, axis=0, keepdims=True)
        for d in range(owners):
            for c in range(tiles):
                lanes = (d * tiles + c) * 128
                parts_ref[j * owners + d, c : c + 1, :] = total[:, lanes : lanes + 128]
        return carry

    lax.fori_loop(0, chunks, finish, 0)
    stores = [
        pltpu.make_async_copy(out_ref, out_hbm, load_sems.at[0]),
        pltpu.make_async_copy(effect_ref, effect_hbm, load_sems.at[1]),
    ]
    for store in stores:
        store.start()
    for copy in hand_out(parts_ref, sums_ref, send_sems, recv_sems, 6):
        copy.wait()
    score_ref[...] = jnp.sum(sums_ref[...], axis=0)
    for store in stores:
        store.wait()


def on_device(features, base_rows, positions, alt_bases, decay_rate, residue, skip_gain):
    length, _, width = features.shape
    devices = lax.axis_size("context")
    nv = positions.shape[0] // devices
    share = width // devices
    tiles = share // 128
    half = length // 2
    table = cheb_table(length)

    gm = jnp.asarray(split3_lhs(pad_rows(table[::-1, :KD].T, 16)))
    lag = np.arange(half)[:, None] - np.arange(half)[None]
    toeplitz = np.where((lag >= 0)[None], table[np.maximum(lag, 0), :KB].transpose(2, 0, 1), 0.0)
    toeplitz = toeplitz.reshape(KB * half, half)
    ends = pad_rows(table[:half, :KB][::-1].T, 8)
    gb = jnp.asarray(split3_lhs(np.concatenate([toeplitz, ends], axis=0)))
    gx = jnp.asarray(split3_lhs(pad_cols(table[:half, :KB], 16)))
    gd = jnp.asarray(split3_lhs(pad_cols(table[:, :KD], 16)))

    operands = (
        positions, alt_bases, gm, gb, gx, gd, features.transpose(1, 0, 2), base_rows.transpose(1, 0, 2),
        decay_rate, residue, skip_gain.reshape(1, width),
    )
    vmem = pl.BlockSpec(memory_space=pltpu.VMEM)
    ref_out, effect, channel_score = pl.pallas_call(
        functools.partial(kernel, nv),
        in_specs=[pl.BlockSpec(memory_space=pltpu.HBM)] * 11,
        out_specs=[pl.BlockSpec(memory_space=pltpu.HBM)] * 2 + [vmem],
        out_shape=[
            jax.ShapeDtypeStruct((length, width), BF16),
            jax.ShapeDtypeStruct((length, width), BF16),
            jax.ShapeDtypeStruct((tiles, 128), F32),
        ],
        scratch_shapes=[pltpu.VMEM((length, width), BF16) for _ in range(2)]
        + [pltpu.SMEM(a.shape, a.dtype) for a in operands[:2]]
        + [pltpu.VMEM(a.shape, a.dtype) for a in operands[2:]]
        + [
            pltpu.SemaphoreType.DMA((13,)),
            pltpu.VMEM((devices, tiles * (KF + nv), 128), F32),
            pltpu.VMEM((devices, tiles * (KF + nv), 128), F32),
            pltpu.VMEM((devices, tiles * 2 * KF, 128), F32),
            pltpu.VMEM((devices, tiles * 2 * KF, 128), F32),
            pltpu.VMEM((devices, tiles * (KD - KF), 128), BF16),
            pltpu.VMEM((devices, tiles * (KD - KF), 128), BF16),
            pltpu.VMEM((devices, tiles * 2 * (KD - KF), 128), BF16),
            pltpu.VMEM((devices, tiles * 2 * (KD - KF), 128), BF16),
            pltpu.VMEM((devices, tiles * (KD - KF), 128), F32),
            pltpu.VMEM((devices, tiles * 2 * (KD - KF), 128), F32),
            pltpu.VMEM((length, width), F32),
            pltpu.VMEM((length, width), F32),
            pltpu.VMEM((4, 2 * length, 128), F32),
            pltpu.VMEM((devices, tiles, 128), F32),
            pltpu.VMEM((devices, tiles, 128), F32),
            pltpu.SemaphoreType.DMA((7, devices)),
            pltpu.SemaphoreType.DMA((7, devices)),
        ],
        compiler_params=pltpu.CompilerParams(
            collective_id=0, has_side_effects=True
        ),
        name="score_variants",
    )(*operands)
    return ref_out, effect, channel_score.reshape(share)


def solution(mesh):
    return jax.shard_map(
        on_device,
        mesh=mesh,
        in_specs=(P(("group", "context"), None, None), P(), P("group"), P("group"), P(), P(), P()),
        out_specs=(
            P(("group", "context"), None),
            P(("group", "context"), None),
            P(("group", "context")),
        ),
        check_vma=False,
    )
```
